512 devices in a mesh: head: 16 (over x_lo, y), blk: 32 (over z, x_hi, core).
Axes of the slice: x: 4 (x_hi: 2, x_lo: 2; x = x_hi * 2 + x_lo), y: 8, z: 8, core: 2. Of those that a mesh axis runs over, the one named last changes fastest.
Arguments:
- query: bfloat16 [65536, 2048], P(('blk', 'head')), may hold values from -8 to 8
- key_in: bfloat16 [65536, 2048], P(('blk', 'head')), may hold values from -8 to 8
- value: bfloat16 [65536, 2048], P(('blk', 'head')), may hold values from -6 to 6
- grad_out: bfloat16 [65536, 2048], P(('blk', 'head')), may hold values from -96 to 96
Outputs:
- grad_query: bfloat16 [65536, 2048], P(('blk', 'head'))
- grad_key: bfloat16 [65536, 2048], P(('blk', 'head'))
- grad_value: bfloat16 [65536, 2048], P(('blk', 'head'))
The draws below stay inside these ranges and needn't reach their ends.
All inputs are finite; a program needn't handle non-finite values.
Results may differ from the reference program's by a relative error of at most 0.0052.
Values may be sent and summed in bfloat16 or wider, within the bound.
A program may use at most 64 MiB of HBM per device.

```python
import math
import jax
import jax.numpy as jnp
from jax import lax

HEADS = 16
HEAD_DIM = 128
D = 2048
HALF = 512
TILE = 512
SEQ = 65536


def query_key_pair(key):
    base_key = jax.random.fold_in(key, 1234)
    key_first, key_second, key_third, key_fourth = jax.random.split(base_key, 4)
    log_low = math.log(0.5)
    log_high = math.log(2.0)
    query_rows = jnp.exp(jax.random.uniform(key_third, (SEQ, 1), jnp.float32, log_low, log_high))
    key_rows = jnp.exp(jax.random.uniform(key_fourth, (SEQ, 1), jnp.float32, log_low, log_high))
    queries = jnp.clip(jax.random.normal(key_first, (SEQ, D), jnp.float32), -3.0, 3.0) * query_rows
    keys_all = jnp.clip(jax.random.normal(key_second, (SEQ, D), jnp.float32), -3.0, 3.0) * key_rows
    return (queries, keys_all)


def draw_query(key, part):
    return query_key_pair(key)[0].astype(jnp.bfloat16)


def draw_key_in(key, part):
    return query_key_pair(key)[1].astype(jnp.bfloat16)


def levels(stream_key, extent, cuts, smallest, top_value):
    loudness = 1.0
    for position, shards_of in cuts:
        steps = jax.random.uniform(jax.random.fold_in(jax.random.fold_in(stream_key, 6), position), (shards_of,), jnp.float32, smallest / len(cuts), top_value / len(cuts))
        loudness = loudness * jnp.repeat(jnp.exp(steps), extent[position] // shards_of).reshape((-1,) + (1,) * (len(extent) - 1 - position))
    return loudness


def centred(key, extent, scale, bound, cuts=(), held_as=jnp.bfloat16):
    values = scale * jax.random.normal(key, extent, jnp.float32)
    if cuts:
        values = values * levels(key, extent, cuts, -0.22, 0.18)
    return jnp.clip(values, -bound, bound).astype(held_as)


def setup_inputs(seed: int = 0) -> dict:
    key_of = jax.random.split(jax.random.key(seed), 5)
    query = draw_query(jax.random.fold_in(key_of[4], 71), 0)
    key_in = draw_key_in(jax.random.fold_in(key_of[4], 71), 0)
    value = centred(key_of[2], (SEQ, D), 1.0, 6.0, ((0, 512),))
    grad_out = centred(key_of[3], (SEQ, D), (max(1, HALF // 32)), 96.0, ((0, 512),))
    return dict(query=query, key_in=key_in, value=value, grad_out=grad_out)


def head_grads(operands):
    query_h, key_h, value_h, grad_h = operands
    score_scale = HEAD_DIM ** -0.5
    key_span = TILE + 2 * HALF
    padding = jnp.zeros((HALF, HEAD_DIM), key_h.dtype)
    key_pad = jnp.concatenate([padding, key_h, padding], axis=0)
    value_pad = jnp.concatenate([padding, value_h, padding], axis=0)
    row_ids = jnp.arange(TILE, dtype=jnp.int32)[:, None]
    col_ids = jnp.arange(key_span, dtype=jnp.int32)[None, :]

    def query_block(state, index):
        grad_key, grad_value = state
        offset = (index * TILE).astype(jnp.int32)
        query_part = lax.dynamic_slice_in_dim(query_h, offset, TILE, 0)
        grad_part = lax.dynamic_slice_in_dim(grad_h, offset, TILE, 0)
        key_part = lax.dynamic_slice_in_dim(key_pad, offset, key_span, 0)
        value_part = lax.dynamic_slice_in_dim(value_pad, offset, key_span, 0)
        key_pos = offset - HALF + col_ids
        query_pos = offset + row_ids
        within = (jnp.abs(query_pos - key_pos) <= HALF) & (key_pos >= 0) & (key_pos < SEQ)
        raw = jnp.dot(query_part, key_part.T, preferred_element_type=jnp.float32) * score_scale
        scores = jnp.where(within, raw, -1e30)
        row_max = jnp.max(scores, axis=1, keepdims=True)
        shifted = jnp.exp(scores - row_max)
        denominator = jnp.sum(shifted, axis=1, keepdims=True)
        output_rows = jnp.dot(shifted.astype(jnp.bfloat16), value_part, preferred_element_type=jnp.float32) / denominator
        log_total = row_max + jnp.log(denominator)
        row_delta = jnp.sum(grad_part.astype(jnp.float32) * output_rows, axis=1, keepdims=True)
        weights = jnp.exp(scores - log_total)
        grad_weights = jnp.dot(grad_part, value_part.T, preferred_element_type=jnp.float32)
        grad_scores = weights * (grad_weights - row_delta)
        weights_low = weights.astype(jnp.bfloat16)
        scores_low = grad_scores.astype(jnp.bfloat16)
        add_value = jnp.dot(weights_low.T, grad_part, preferred_element_type=jnp.float32)
        add_key = jnp.dot(scores_low.T, query_part, preferred_element_type=jnp.float32) * score_scale
        grad_query = jnp.dot(scores_low, key_part, preferred_element_type=jnp.float32) * score_scale
        old_key = lax.dynamic_slice_in_dim(grad_key, offset, key_span, 0)
        old_value = lax.dynamic_slice_in_dim(grad_value, offset, key_span, 0)
        grad_key = lax.dynamic_update_slice_in_dim(grad_key, old_key + add_key, offset, 0)
        grad_value = lax.dynamic_update_slice_in_dim(grad_value, old_value + add_value, offset, 0)
        return (grad_key, grad_value), grad_query

    zeros_f32 = jnp.zeros((SEQ + 2 * HALF, HEAD_DIM), jnp.float32)
    tile_ids = jnp.arange(SEQ // TILE, dtype=jnp.int32)
    (grad_key, grad_value), query_parts = lax.scan(query_block, (zeros_f32, zeros_f32), tile_ids)
    grad_query = query_parts.reshape(SEQ, HEAD_DIM)
    grad_key = grad_key[HALF:HALF + SEQ]
    grad_value = grad_value[HALF:HALF + SEQ]
    return grad_query.astype(jnp.bfloat16), grad_key.astype(jnp.bfloat16), grad_value.astype(jnp.bfloat16)


def by_head(matrix):
    return jnp.transpose(matrix.reshape(SEQ, HEADS, HEAD_DIM), (1, 0, 2))


def by_token(stacked):
    return jnp.transpose(stacked, (1, 0, 2)).reshape(SEQ, D)


def reference(query, key_in, value, grad_out):
    results = lax.map(head_grads, (by_head(query), by_head(key_in), by_head(value), by_head(grad_out)))
    return by_token(results[0]), by_token(results[1]), by_token(results[2])
```

```python
import functools

import jax
import jax.numpy as jnp
from jax import lax
from jax.experimental import pallas as pl
from jax.experimental.pallas import tpu as pltpu
from jax.sharding import PartitionSpec as P

HEADS = 16
DIM = 128
HALF = 512
T = 256
CHUNKS = (T + 2 * HALF) // T
LOG2E = 1.4426950408889634
MESH = pl.DeviceIdType.MESH


def dot_nt(a, b):
    return lax.dot_general(a, b, (((1,), (1,)), ((), ())), preferred_element_type=jnp.float32)


def dot_nn(a, b):
    return jnp.dot(a, b, preferred_element_type=jnp.float32)


def kernel(
    heads, blks, part,
    q_in, k_in, v_in, g_in, dq_out, dk_out, dv_out,
    q_t, g_t, k_e, v_e, k_tr, s_buf, d_buf, dk_acc, dv_acc, dq_t, dk_t, dv_t, half_out, half_in,
    send, recv, hsend, hrecv, gsend, grecv, local,
):
    rows = heads * part
    tiles = rows // T
    scale = DIM ** (-0.5)
    me = lax.axis_index("head")
    blk = lax.axis_index("blk")
    left = lax.rem(blk + blks - 1, blks)
    right = lax.rem(blk + 1, blks)

    barrier = pltpu.get_barrier_semaphore()

    def greet(d, carry):
        pl.semaphore_signal(barrier, inc=1, device_id={"head": lax.rem(me + d, heads)}, device_id_type=MESH)
        return carry

    lax.fori_loop(1, heads, greet, 0)
    pl.semaphore_signal(barrier, inc=1, device_id={"blk": left}, device_id_type=MESH)
    pl.semaphore_signal(barrier, inc=1, device_id={"blk": right}, device_id_type=MESH)
    pl.semaphore_wait(barrier, heads + 1)

    def lanes(index):
        return pl.ds(pl.multiple_of(index * DIM, DIM), DIM)

    def span(index, base=0):
        return pl.ds(pl.multiple_of(base + index * part, part), part)

    ins = ((k_in, k_e, HALF), (v_in, v_e, HALF), (q_in, q_t, 0), (g_in, g_t, 0))

    def in_copy(n, peer, source):
        src, dst, base = ins[n]
        return pltpu.make_async_remote_copy(
            src_ref=src.at[:, lanes(peer)],
            dst_ref=dst.at[span(source, base)],
            send_sem=send.at[n, peer],
            recv_sem=recv.at[n, source],
            device_id={"head": peer},
            device_id_type=MESH,
        )

    own = []
    for n, (src, dst, base) in enumerate(ins):
        copy = pltpu.make_async_copy(src.at[:, lanes(me)], dst.at[span(me, base)], local.at[n])
        copy.start()
        own.append(copy)

    for n in range(4):
        def start_in(d, carry, n=n):
            in_copy(n, lax.rem(me + d, heads), me).start()
            return carry

        lax.fori_loop(1, heads, start_in, 0)

    def wait_in(n):
        def body(d, carry):
            source = lax.rem(me + d, heads)
            in_copy(n, source, source).wait_recv()
            return carry

        own[n].wait()
        lax.fori_loop(1, heads, body, 0)

    def halo(slot, ext, src_row, dst_row, target):
        return pltpu.make_async_remote_copy(
            src_ref=ext.at[pl.ds(src_row, HALF)],
            dst_ref=ext.at[pl.ds(dst_row, HALF)],
            send_sem=hsend.at[slot],
            recv_sem=hrecv.at[slot],
            device_id={"blk": target},
            device_id_type=MESH,
        )

    halos = []
    for n, ext in ((0, k_e), (1, v_e)):
        wait_in(n)
        halos.append(halo(2 * n, ext, rows, 0, right))
        halos.append(halo(2 * n + 1, ext, HALF, HALF + rows, left))
        halos[-2].start()
        halos[-1].start()

    dk_acc[...] = jnp.zeros_like(dk_acc)
    dv_acc[...] = jnp.zeros_like(dv_acc)
    for copy in halos:
        copy.wait_recv()

    def turn(c, carry):
        k_tr[c] = k_e[pl.ds(pl.multiple_of(c * T, T), T), :].astype(jnp.float32).T.astype(jnp.bfloat16)
        return carry

    lax.fori_loop(0, tiles + CHUNKS - 1, turn, 0)
    wait_in(2)
    wait_in(3)

    def out_copy(n, src, dst, peer, source):
        return pltpu.make_async_remote_copy(
            src_ref=src.at[span(peer)],
            dst_ref=dst.at[:, lanes(source)],
            send_sem=send.at[n, peer],
            recv_sem=recv.at[n, source],
            device_id={"head": peer},
            device_id_type=MESH,
        )

    outs = ((4, dq_t, dq_out), (5, dk_t, dk_out), (6, dv_t, dv_out))

    def give(index, peer):
        n, src, dst = outs[index]

        @pl.when(peer != me)
        def _():
            out_copy(n, src, dst, peer, me).start()

        @pl.when(peer == me)
        def _():
            pltpu.make_async_copy(src.at[span(me)], dst.at[:, lanes(me)], local.at[n]).start()

    def send_query(i):
        t = lax.rem(i + me, tiles)
        for half in range(T // part):
            give(0, t * (T // part) + half)

    row = lax.broadcasted_iota(jnp.int32, (T, T), 0)
    col = lax.broadcasted_iota(jnp.int32, (T, T), 1)
    seq_total = rows * blks
    fold = scale * LOG2E

    def tile_step(i, carry):
        t = lax.rem(i + me, tiles)
        offset = pl.multiple_of(t * T, T)
        q = q_t[pl.ds(offset, T), :]
        g = g_t[pl.ds(offset, T), :]
        top = jnp.full((1, T), -1e30, jnp.float32)
        biases = []
        for c in range(CHUNKS):
            keys = pl.ds(pl.multiple_of(offset + c * T, T), T)
            s = dot_nt(k_e[keys, :], q)
            if c == 0:
                s = jnp.where(row >= col, s, -1e30)
            if c == CHUNKS - 1:
                s = jnp.where(row <= col, s, -1e30)
            first = blk * rows + offset + (c * T - HALF)
            bias = jnp.where((first >= 0) & (first < seq_total), 0.0, 1e30).astype(jnp.float32)
            biases.append(bias)
            top = jnp.maximum(top, jnp.max(s, axis=0, keepdims=True) - bias)
            s_buf[c] = s
        total = jnp.zeros((1, T), jnp.float32)
        delta = jnp.zeros((1, T), jnp.float32)
        for c in range(CHUNKS):
            keys = pl.ds(pl.multiple_of(offset + c * T, T), T)
            p = jnp.exp2((s_buf[c] - (top + biases[c])) * fold)
            dp = dot_nt(v_e[keys, :], g)
            total = total + jnp.sum(p, axis=0, keepdims=True)
            delta = delta + jnp.sum(p * dp, axis=0, keepdims=True)
            s_buf[c] = p
            d_buf[c] = dp
        inv = 1.0 / total
        delta = delta * inv
        dq = jnp.zeros((DIM, T), jnp.float32)
        for c in range(CHUNKS):
            keys = pl.ds(pl.multiple_of(offset + c * T, T), T)
            w = s_buf[c] * inv
            ds = (w * (d_buf[c] - delta)).astype(jnp.bfloat16)
            dv_acc[keys, :] += dot_nn(w.astype(jnp.bfloat16), g)
            dk_acc[keys, :] += dot_nn(ds, q)
            dq = dq + dot_nn(k_tr[t + c], ds)
        dq_t[pl.ds(offset, T), :] = (dq * scale).T.astype(jnp.bfloat16)

        @pl.when(i > 0)
        def _():
            send_query(i - 1)

        return carry

    lax.fori_loop(0, tiles, tile_step, 0)

    for slot, acc, at, factor in (
        (0, dk_acc, 0, scale), (1, dv_acc, 0, 1.0),
        (2, dk_acc, HALF + rows, scale), (3, dv_acc, HALF + rows, 1.0),
    ):
        half_out[slot] = (acc[pl.ds(at, HALF), :] * factor).astype(jnp.bfloat16)
    send_query(tiles - 1)
    mid = rows - 2 * HALF
    dk_t[pl.ds(HALF, mid), :] = (dk_acc[pl.ds(2 * HALF, mid), :] * scale).astype(jnp.bfloat16)
    dv_t[pl.ds(HALF, mid), :] = dv_acc[pl.ds(2 * HALF, mid), :].astype(jnp.bfloat16)
    backs = []
    for slot in range(4):
        copy = pltpu.make_async_remote_copy(
            src_ref=half_out.at[slot],
            dst_ref=half_in.at[slot],
            send_sem=gsend.at[slot],
            recv_sem=grecv.at[slot],
            device_id={"blk": left if slot < 2 else right},
            device_id_type=MESH,
        )
        copy.start()
        backs.append(copy)

    edge = HALF // part
    inner = heads - 2 * edge

    def send_inner(d, carry):
        peer = edge + lax.rem(me + d, inner)
        give(1, peer)
        give(2, peer)
        return carry

    lax.fori_loop(0, inner, send_inner, 0)
    for copy in backs:
        copy.wait_recv()
    for slot, at, out, acc, factor in (
        (0, rows - HALF, dk_t, dk_acc, scale), (1, rows - HALF, dv_t, dv_acc, 1.0),
        (2, 0, dk_t, dk_acc, scale), (3, 0, dv_t, dv_acc, 1.0),
    ):
        mine = acc[pl.ds(at + HALF, HALF), :] * factor
        out[pl.ds(at, HALF), :] = (mine + half_in[slot].astype(jnp.float32)).astype(jnp.bfloat16)

    def send_outer(d, carry):
        peer = lax.rem(heads - edge + lax.rem(me + d, 2 * edge), heads)
        give(1, peer)
        give(2, peer)
        return carry

    lax.fori_loop(0, 2 * edge, send_outer, 0)

    for n, src, dst in outs:
        pltpu.make_async_copy(src.at[span(me)], dst.at[:, lanes(me)], local.at[n]).wait()

    def finish(d, carry):
        other = lax.rem(me + d, heads)
        for n in range(4):
            in_copy(n, other, me).wait_send()
        for n, src, dst in outs:
            out_copy(n, src, dst, other, me).wait_send()
            out_copy(n, src, dst, other, other).wait_recv()
        return carry

    lax.fori_loop(1, heads, finish, 0)
    for copy in halos + backs:
        copy.wait_send()


def shards(query, key_in, value, grad_out):
    heads = lax.axis_size("head")
    blks = lax.axis_size("blk")
    part = query.shape[0]
    rows = heads * part
    wide = rows + 2 * HALF
    bf16, f32 = jnp.bfloat16, jnp.float32
    shape = jax.ShapeDtypeStruct(query.shape, bf16)
    any_spec = pl.BlockSpec(memory_space=pl.ANY)
    dma = pltpu.SemaphoreType.DMA
    return pl.pallas_call(
        functools.partial(kernel, heads, blks, part),
        out_shape=(shape, shape, shape),
        in_specs=[any_spec] * 4,
        out_specs=(any_spec,) * 3,
        scratch_shapes=[
            pltpu.VMEM((rows, DIM), bf16),
            pltpu.VMEM((rows, DIM), bf16),
            pltpu.VMEM((wide, DIM), bf16),
            pltpu.VMEM((wide, DIM), bf16),
            pltpu.VMEM((wide // T, DIM, T), bf16),
            pltpu.VMEM((CHUNKS, T, T), f32),
            pltpu.VMEM((CHUNKS, T, T), f32),
            pltpu.VMEM((wide, DIM), f32),
            pltpu.VMEM((wide, DIM), f32),
            pltpu.VMEM((rows, DIM), bf16),
            pltpu.VMEM((rows, DIM), bf16),
            pltpu.VMEM((rows, DIM), bf16),
            pltpu.VMEM((4, HALF, DIM), bf16),
            pltpu.VMEM((4, HALF, DIM), bf16),
            dma((7, heads)),
            dma((7, heads)),
            dma((4,)),
            dma((4,)),
            dma((4,)),
            dma((4,)),
            dma((7,)),
        ],
        compiler_params=pltpu.CompilerParams(collective_id=0, has_side_effects=True),
    )(query, key_in, value, grad_out)


def solution(mesh):
    placed = P(("blk", "head"), None)
    return jax.shard_map(
        shards,
        mesh=mesh,
        in_specs=(placed,) * 4,
        out_specs=(placed,) * 3,
        check_vma=False,
    )
```

```python
import functools

import jax
import jax.numpy as jnp
from jax import lax
from jax.experimental import pallas as pl
from jax.experimental.pallas import tpu as pltpu
from jax.sharding import PartitionSpec as P

HEADS = 16
DIM = 128
HALF = 512
T = 256
CHUNKS = (T + 2 * HALF) // T
LOG2E = 1.4426950408889634
MESH = pl.DeviceIdType.MESH


def dot_nt(a, b):
    return lax.dot_general(a, b, (((1,), (1,)), ((), ())), preferred_element_type=jnp.float32)


def dot_nn(a, b):
    return jnp.dot(a, b, preferred_element_type=jnp.float32)


def kernel(
    heads, blks, part,
    q_in, k_in, v_in, g_in, dq_out, dk_out, dv_out,
    q_t, g_t, k_e, v_e, k_tr, s_buf, d_buf, inv_buf, dk_acc, dv_acc, dq_t, dk_t, dv_t, half_out, half_in,
    send, recv, hsend, hrecv, gsend, grecv, local,
):
    rows = heads * part
    tiles = rows // T
    scale = DIM ** (-0.5)
    me = lax.axis_index("head")
    blk = lax.axis_index("blk")
    left = lax.rem(blk + blks - 1, blks)
    right = lax.rem(blk + 1, blks)

    barrier = pltpu.get_barrier_semaphore()

    def greet(d, carry):
        pl.semaphore_signal(barrier, inc=1, device_id={"head": lax.rem(me + d, heads)}, device_id_type=MESH)
        return carry

    lax.fori_loop(1, heads, greet, 0)
    pl.semaphore_signal(barrier, inc=1, device_id={"blk": left}, device_id_type=MESH)
    pl.semaphore_signal(barrier, inc=1, device_id={"blk": right}, device_id_type=MESH)
    pl.semaphore_wait(barrier, heads + 1)

    def lanes(index):
        return pl.ds(pl.multiple_of(index * DIM, DIM), DIM)

    def span(index, base=0):
        return pl.ds(pl.multiple_of(base + index * part, part), part)

    ins = ((k_in, k_e, HALF), (q_in, q_t, 0), (v_in, v_e, HALF), (g_in, g_t, 0))

    def in_copy(n, peer, source):
        src, dst, base = ins[n]
        return pltpu.make_async_remote_copy(
            src_ref=src.at[:, lanes(peer)],
            dst_ref=dst.at[span(source, base)],
            send_sem=send.at[n, peer],
            recv_sem=recv.at[n, source],
            device_id={"head": peer},
            device_id_type=MESH,
        )

    own = []
    for n, (src, dst, base) in enumerate(ins):
        copy = pltpu.make_async_copy(src.at[:, lanes(me)], dst.at[span(me, base)], local.at[n])
        copy.start()
        own.append(copy)

    for n in range(4):
        def start_in(d, carry, n=n):
            in_copy(n, lax.rem(me + d, heads), me).start()
            return carry

        lax.fori_loop(1, heads, start_in, 0)

    def wait_in(n):
        def body(d, carry):
            source = lax.rem(me + d, heads)
            in_copy(n, source, source).wait_recv()
            return carry

        own[n].wait()
        lax.fori_loop(1, heads, body, 0)

    def halo(slot, ext, src_row, dst_row, target):
        return pltpu.make_async_remote_copy(
            src_ref=ext.at[pl.ds(src_row, HALF)],
            dst_ref=ext.at[pl.ds(dst_row, HALF)],
            send_sem=hsend.at[slot],
            recv_sem=hrecv.at[slot],
            device_id={"blk": target},
            device_id_type=MESH,
        )

    def spread(n, slot, ext):
        wait_in(n)
        pair = [halo(slot, ext, rows, 0, right), halo(slot + 1, ext, HALF, HALF + rows, left)]
        for copy in pair:
            copy.start()
        return pair

    key_halos = spread(0, 0, k_e)
    dk_acc[...] = jnp.zeros_like(dk_acc)
    dv_acc[...] = jnp.zeros_like(dv_acc)
    for copy in key_halos:
        copy.wait_recv()

    def turn(c, carry):
        k_tr[c] = k_e[pl.ds(pl.multiple_of(c * T, T), T), :].astype(jnp.float32).T.astype(jnp.bfloat16)
        return carry

    lax.fori_loop(0, tiles + CHUNKS - 1, turn, 0)
    wait_in(1)

    def out_copy(n, src, dst, peer, source):
        return pltpu.make_async_remote_copy(
            src_ref=src.at[span(peer)],
            dst_ref=dst.at[:, lanes(source)],
            send_sem=send.at[n, peer],
            recv_sem=recv.at[n, source],
            device_id={"head": peer},
            device_id_type=MESH,
        )

    outs = ((4, dq_t, dq_out), (5, dk_t, dk_out), (6, dv_t, dv_out))

    def give(index, peer):
        n, src, dst = outs[index]

        @pl.when(peer != me)
        def _():
            out_copy(n, src, dst, peer, me).start()

        @pl.when(peer == me)
        def _():
            pltpu.make_async_copy(src.at[span(me)], dst.at[:, lanes(me)], local.at[n]).start()

    def send_query(i):
        t = lax.rem(i + me, tiles)
        for half in range(T // part):
            give(0, t * (T // part) + half)

    row = lax.broadcasted_iota(jnp.int32, (T, T), 0)
    col = lax.broadcasted_iota(jnp.int32, (T, T), 1)
    seq_total = rows * blks
    fold = scale * LOG2E

    def score_step(t, carry):
        offset = pl.multiple_of(t * T, T)
        q = q_t[pl.ds(offset, T), :]
        top = jnp.full((1, T), -1e30, jnp.float32)
        biases, parts = [], []
        for c in range(CHUNKS):
            keys = pl.ds(pl.multiple_of(offset + c * T, T), T)
            s = dot_nt(k_e[keys, :], q)
            if c == 0:
                s = jnp.where(row >= col, s, -1e30)
            if c == CHUNKS - 1:
                s = jnp.where(row <= col, s, -1e30)
            first = blk * rows + offset + (c * T - HALF)
            bias = jnp.where((first >= 0) & (first < seq_total), 0.0, 1e30).astype(jnp.float32)
            biases.append(bias)
            top = jnp.maximum(top, jnp.max(s, axis=0, keepdims=True) - bias)
            parts.append(s)
        total = jnp.zeros((1, T), jnp.float32)
        for c in range(CHUNKS):
            p = jnp.exp2((parts[c] - (top + biases[c])) * fold)
            total = total + jnp.sum(p, axis=0, keepdims=True)
            s_buf[t, c] = p
        inv_buf[t] = 1.0 / total
        return carry

    lax.fori_loop(0, tiles, score_step, 0)

    value_halos = spread(2, 2, v_e)
    for copy in value_halos:
        copy.wait_recv()
    wait_in(3)
    halos = key_halos + value_halos

    def tile_step(i, carry):
        t = lax.rem(i + me, tiles)
        offset = pl.multiple_of(t * T, T)
        q = q_t[pl.ds(offset, T), :]
        g = g_t[pl.ds(offset, T), :]
        inv = inv_buf[t]
        delta = jnp.zeros((1, T), jnp.float32)
        for c in range(CHUNKS):
            keys = pl.ds(pl.multiple_of(offset + c * T, T), T)
            dp = dot_nt(v_e[keys, :], g)
            delta = delta + jnp.sum(s_buf[t, c] * dp, axis=0, keepdims=True)
            d_buf[c] = dp
        delta = delta * inv
        dq = jnp.zeros((DIM, T), jnp.float32)
        for c in range(CHUNKS):
            keys = pl.ds(pl.multiple_of(offset + c * T, T), T)
            w = s_buf[t, c] * inv
            ds = (w * (d_buf[c] - delta)).astype(jnp.bfloat16)
            dv_acc[keys, :] += dot_nn(w.astype(jnp.bfloat16), g)
            dk_acc[keys, :] += dot_nn(ds, q)
            dq = dq + dot_nn(k_tr[t + c], ds)
        dq_t[pl.ds(offset, T), :] = (dq * scale).T.astype(jnp.bfloat16)

        @pl.when(i > 0)
        def _():
            send_query(i - 1)

        return carry

    lax.fori_loop(0, tiles, tile_step, 0)

    for slot, acc, at, factor in (
        (0, dk_acc, 0, scale), (1, dv_acc, 0, 1.0),
        (2, dk_acc, HALF + rows, scale), (3, dv_acc, HALF + rows, 1.0),
    ):
        half_out[slot] = (acc[pl.ds(at, HALF), :] * factor).astype(jnp.bfloat16)
    send_query(tiles - 1)
    mid = rows - 2 * HALF
    dk_t[pl.ds(HALF, mid), :] = (dk_acc[pl.ds(2 * HALF, mid), :] * scale).astype(jnp.bfloat16)
    dv_t[pl.ds(HALF, mid), :] = dv_acc[pl.ds(2 * HALF, mid), :].astype(jnp.bfloat16)
    backs = []
    for slot in range(4):
        copy = pltpu.make_async_remote_copy(
            src_ref=half_out.at[slot],
            dst_ref=half_in.at[slot],
            send_sem=gsend.at[slot],
            recv_sem=grecv.at[slot],
            device_id={"blk": left if slot < 2 else right},
            device_id_type=MESH,
        )
        copy.start()
        backs.append(copy)

    edge = HALF // part
    inner = heads - 2 * edge

    def send_inner(d, carry):
        peer = edge + lax.rem(me + d, inner)
        give(1, peer)
        give(2, peer)
        return carry

    lax.fori_loop(0, inner, send_inner, 0)
    for copy in backs:
        copy.wait_recv()
    for slot, at, out, acc, factor in (
        (0, rows - HALF, dk_t, dk_acc, scale), (1, rows - HALF, dv_t, dv_acc, 1.0),
        (2, 0, dk_t, dk_acc, scale), (3, 0, dv_t, dv_acc, 1.0),
    ):
        mine = acc[pl.ds(at + HALF, HALF), :] * factor
        out[pl.ds(at, HALF), :] = (mine + half_in[slot].astype(jnp.float32)).astype(jnp.bfloat16)

    def send_outer(d, carry):
        peer = lax.rem(heads - edge + lax.rem(me + d, 2 * edge), heads)
        give(1, peer)
        give(2, peer)
        return carry

    lax.fori_loop(0, 2 * edge, send_outer, 0)

    for n, src, dst in outs:
        pltpu.make_async_copy(src.at[span(me)], dst.at[:, lanes(me)], local.at[n]).wait()

    def finish(d, carry):
        other = lax.rem(me + d, heads)
        for n in range(4):
            in_copy(n, other, me).wait_send()
        for n, src, dst in outs:
            out_copy(n, src, dst, other, me).wait_send()
            out_copy(n, src, dst, other, other).wait_recv()
        return carry

    lax.fori_loop(1, heads, finish, 0)
    for copy in halos + backs:
        copy.wait_send()


def settle(*refs):
    froms, tos, holds = refs[:3], refs[3:6], refs[6:9]
    into, onto = refs[9:]
    reads = [pltpu.make_async_copy(a, b, into.at[i]) for i, (a, b) in enumerate(zip(froms, holds))]
    writes = [pltpu.make_async_copy(b, c, onto.at[i]) for i, (b, c) in enumerate(zip(holds, tos))]
    for read in reads:
        read.start()
    for read, write in zip(reads, writes):
        read.wait()
        write.start()
    for write in writes:
        write.wait()


def shards(query, key_in, value, grad_out):
    heads = lax.axis_size("head")
    blks = lax.axis_size("blk")
    part = query.shape[0]
    rows = heads * part
    wide = rows + 2 * HALF
    bf16, f32 = jnp.bfloat16, jnp.float32
    shape = jax.ShapeDtypeStruct(query.shape, bf16)
    any_spec = pl.BlockSpec(memory_space=pl.ANY)
    dma = pltpu.SemaphoreType.DMA
    grads = pl.pallas_call(
        functools.partial(kernel, heads, blks, part),
        out_shape=(shape, shape, shape),
        in_specs=[any_spec] * 4,
        out_specs=(any_spec,) * 3,
        scratch_shapes=[
            pltpu.VMEM((rows, DIM), bf16),
            pltpu.VMEM((rows, DIM), bf16),
            pltpu.VMEM((wide, DIM), bf16),
            pltpu.VMEM((wide, DIM), bf16),
            pltpu.VMEM((wide // T, DIM, T), bf16),
            pltpu.VMEM((rows // T, CHUNKS, T, T), f32),
            pltpu.VMEM((CHUNKS, T, T), f32),
            pltpu.VMEM((rows // T, 1, T), f32),
            pltpu.VMEM((wide, DIM), f32),
            pltpu.VMEM((wide, DIM), f32),
            pltpu.VMEM((rows, DIM), bf16),
            pltpu.VMEM((rows, DIM), bf16),
            pltpu.VMEM((rows, DIM), bf16),
            pltpu.VMEM((4, HALF, DIM), bf16),
            pltpu.VMEM((4, HALF, DIM), bf16),
            dma((7, heads)),
            dma((7, heads)),
            dma((4,)),
            dma((4,)),
            dma((4,)),
            dma((4,)),
            dma((7,)),
        ],
        compiler_params=pltpu.CompilerParams(collective_id=0, has_side_effects=True),
    )(query, key_in, value, grad_out)
    return pl.pallas_call(
        settle,
        out_shape=(shape, shape, shape),
        in_specs=[any_spec] * 3,
        out_specs=(any_spec,) * 3,
        scratch_shapes=[pltpu.VMEM(query.shape, bf16)] * 3 + [dma((3,)), dma((3,))],
    )(*grads)


def solution(mesh):
    placed = P(("blk", "head"), None)
    return jax.shard_map(
        shards,
        mesh=mesh,
        in_specs=(placed,) * 4,
        out_specs=(placed,) * 3,
        check_vma=False,
    )
```

```python
import functools

import jax
import jax.numpy as jnp
from jax import lax
from jax.experimental import pallas as pl
from jax.experimental.pallas import tpu as pltpu
from jax.sharding import PartitionSpec as P

HEADS = 16
DIM = 128
HALF = 512
T = 256
CHUNKS = (T + 2 * HALF) // T
LOG2E = 1.4426950408889634
MESH = pl.DeviceIdType.MESH


def dot_nt(a, b):
    return lax.dot_general(a, b, (((1,), (1,)), ((), ())), preferred_element_type=jnp.float32)


def dot_nn(a, b):
    return jnp.dot(a, b, preferred_element_type=jnp.float32)


def kernel(
    heads, blks, part,
    q_in, k_in, v_in, g_in, dq_out, dk_out, dv_out,
    q_t, g_t, k_e, v_e, k_tr, s_buf, d_buf, inv_buf, dk_acc, dv_acc, dq_t, dk_t, dv_t, half_out, half_in,
    send, recv, hsend, hrecv, gsend, grecv, local,
):
    rows = heads * part
    tiles = rows // T
    scale = DIM ** (-0.5)
    me = lax.axis_index("head")
    blk = lax.axis_index("blk")
    left = lax.rem(blk + blks - 1, blks)
    right = lax.rem(blk + 1, blks)

    barrier = pltpu.get_barrier_semaphore()

    def greet(d, carry):
        pl.semaphore_signal(barrier, inc=1, device_id={"head": lax.rem(me + d, heads)}, device_id_type=MESH)
        return carry

    lax.fori_loop(1, heads, greet, 0)
    pl.semaphore_signal(barrier, inc=1, device_id={"blk": left}, device_id_type=MESH)
    pl.semaphore_signal(barrier, inc=1, device_id={"blk": right}, device_id_type=MESH)
    pl.semaphore_wait(barrier, heads + 1)

    def lanes(index):
        return pl.ds(pl.multiple_of(index * DIM, DIM), DIM)

    def span(index, base=0):
        return pl.ds(pl.multiple_of(base + index * part, part), part)

    ins = ((k_in, k_e, HALF), (q_in, q_t, 0), (v_in, v_e, HALF), (g_in, g_t, 0))

    def in_copy(n, peer, source):
        src, dst, base = ins[n]
        return pltpu.make_async_remote_copy(
            src_ref=src.at[:, lanes(peer)],
            dst_ref=dst.at[span(source, base)],
            send_sem=send.at[n, peer],
            recv_sem=recv.at[n, source],
            device_id={"head": peer},
            device_id_type=MESH,
        )

    own = []
    for n, (src, dst, base) in enumerate(ins):
        copy = pltpu.make_async_copy(src.at[:, lanes(me)], dst.at[span(me, base)], local.at[n])
        copy.start()
        own.append(copy)

    for n in range(4):
        def start_in(d, carry, n=n):
            in_copy(n, lax.rem(me + d, heads), me).start()
            return carry

        lax.fori_loop(1, heads, start_in, 0)

    def wait_in(n):
        def body(d, carry):
            source = lax.rem(me + d, heads)
            in_copy(n, source, source).wait_recv()
            return carry

        own[n].wait()
        lax.fori_loop(1, heads, body, 0)

    def halo(slot, ext, src_row, dst_row, target):
        return pltpu.make_async_remote_copy(
            src_ref=ext.at[pl.ds(src_row, HALF)],
            dst_ref=ext.at[pl.ds(dst_row, HALF)],
            send_sem=hsend.at[slot],
            recv_sem=hrecv.at[slot],
            device_id={"blk": target},
            device_id_type=MESH,
        )

    def spread(n, slot, ext):
        wait_in(n)
        pair = [halo(slot, ext, rows, 0, right), halo(slot + 1, ext, HALF, HALF + rows, left)]
        for copy in pair:
            copy.start()
        return pair

    key_halos = spread(0, 0, k_e)
    dk_acc[...] = jnp.zeros_like(dk_acc)
    dv_acc[...] = jnp.zeros_like(dv_acc)
    for copy in key_halos:
        copy.wait_recv()

    def turn(c, carry):
        k_tr[c] = k_e[pl.ds(pl.multiple_of(c * T, T), T), :].astype(jnp.float32).T.astype(jnp.bfloat16)
        return carry

    lax.fori_loop(0, tiles + CHUNKS - 1, turn, 0)
    wait_in(1)

    def out_copy(n, src, dst, peer, source):
        return pltpu.make_async_remote_copy(
            src_ref=src.at[span(peer)],
            dst_ref=dst.at[:, lanes(source)],
            send_sem=send.at[n, peer],
            recv_sem=recv.at[n, source],
            device_id={"head": peer},
            device_id_type=MESH,
        )

    outs = ((4, dq_t, dq_out), (5, dk_t, dk_out), (6, dv_t, dv_out))

    def give(index, peer):
        n, src, dst = outs[index]

        @pl.when(peer != me)
        def _():
            out_copy(n, src, dst, peer, me).start()

        @pl.when(peer == me)
        def _():
            pltpu.make_async_copy(src.at[span(me)], dst.at[:, lanes(me)], local.at[n]).start()

    def pick(i):
        return lax.rem((me + heads - 1) // 2 + tiles - i, tiles)

    def send_query(i):
        t = pick(i)
        for half in range(T // part):
            give(0, t * (T // part) + half)

    row = lax.broadcasted_iota(jnp.int32, (T, T), 0)
    col = lax.broadcasted_iota(jnp.int32, (T, T), 1)
    seq_total = rows * blks
    fold = scale * LOG2E

    def score_step(t, carry):
        offset = pl.multiple_of(t * T, T)
        q = q_t[pl.ds(offset, T), :]
        top = jnp.full((1, T), -1e30, jnp.float32)
        biases, parts = [], []
        for c in range(CHUNKS):
            keys = pl.ds(pl.multiple_of(offset + c * T, T), T)
            s = dot_nt(k_e[keys, :], q)
            if c == 0:
                s = jnp.where(row >= col, s, -1e30)
            if c == CHUNKS - 1:
                s = jnp.where(row <= col, s, -1e30)
            first = blk * rows + offset + (c * T - HALF)
            bias = jnp.where((first >= 0) & (first < seq_total), 0.0, 1e30).astype(jnp.float32)
            biases.append(bias)
            top = jnp.maximum(top, jnp.max(s, axis=0, keepdims=True) - bias)
            parts.append(s)
        total = jnp.zeros((1, T), jnp.float32)
        for c in range(CHUNKS):
            p = jnp.exp2((parts[c] - (top + biases[c])) * fold)
            total = total + jnp.sum(p, axis=0, keepdims=True)
            s_buf[t, c] = p
        inv_buf[t] = 1.0 / total
        return carry

    lax.fori_loop(0, tiles, score_step, 0)

    value_halos = spread(2, 2, v_e)
    for copy in value_halos:
        copy.wait_recv()
    own[3].wait()
    halos = key_halos + value_halos

    def tile_step(i, carry):
        t = pick(i)
        for half in range(T // part):
            source = t * (T // part) + half

            @pl.when(source != me)
            def _():
                in_copy(3, source, source).wait_recv()

        offset = pl.multiple_of(t * T, T)
        q = q_t[pl.ds(offset, T), :]
        g = g_t[pl.ds(offset, T), :]
        inv = inv_buf[t]
        delta = jnp.zeros((1, T), jnp.float32)
        for c in range(CHUNKS):
            keys = pl.ds(pl.multiple_of(offset + c * T, T), T)
            dp = dot_nt(v_e[keys, :], g)
            delta = delta + jnp.sum(s_buf[t, c] * dp, axis=0, keepdims=True)
            d_buf[c] = dp
        delta = delta * inv
        dq = jnp.zeros((DIM, T), jnp.float32)
        for c in range(CHUNKS):
            keys = pl.ds(pl.multiple_of(offset + c * T, T), T)
            w = s_buf[t, c] * inv
            ds = (w * (d_buf[c] - delta)).astype(jnp.bfloat16)
            dv_acc[keys, :] += dot_nn(w.astype(jnp.bfloat16), g)
            dk_acc[keys, :] += dot_nn(ds, q)
            dq = dq + dot_nn(k_tr[t + c], ds)
        dq_t[pl.ds(offset, T), :] = (dq * scale).T.astype(jnp.bfloat16)

        @pl.when(i > 0)
        def _():
            send_query(i - 1)

        return carry

    lax.fori_loop(0, tiles, tile_step, 0)

    for slot, acc, at, factor in (
        (0, dk_acc, 0, scale), (1, dv_acc, 0, 1.0),
        (2, dk_acc, HALF + rows, scale), (3, dv_acc, HALF + rows, 1.0),
    ):
        half_out[slot] = (acc[pl.ds(at, HALF), :] * factor).astype(jnp.bfloat16)
    send_query(tiles - 1)
    mid = rows - 2 * HALF
    dk_t[pl.ds(HALF, mid), :] = (dk_acc[pl.ds(2 * HALF, mid), :] * scale).astype(jnp.bfloat16)
    dv_t[pl.ds(HALF, mid), :] = dv_acc[pl.ds(2 * HALF, mid), :].astype(jnp.bfloat16)
    backs = []
    for slot in range(4):
        copy = pltpu.make_async_remote_copy(
            src_ref=half_out.at[slot],
            dst_ref=half_in.at[slot],
            send_sem=gsend.at[slot],
            recv_sem=grecv.at[slot],
            device_id={"blk": left if slot < 2 else right},
            device_id_type=MESH,
        )
        copy.start()
        backs.append(copy)

    edge = HALF // part
    inner = heads - 2 * edge

    def send_inner(d, carry):
        peer = edge + lax.rem(me + d, inner)
        give(1, peer)
        give(2, peer)
        return carry

    lax.fori_loop(0, inner, send_inner, 0)
    for copy in backs:
        copy.wait_recv()
    for slot, at, out, acc, factor in (
        (0, rows - HALF, dk_t, dk_acc, scale), (1, rows - HALF, dv_t, dv_acc, 1.0),
        (2, 0, dk_t, dk_acc, scale), (3, 0, dv_t, dv_acc, 1.0),
    ):
        mine = acc[pl.ds(at + HALF, HALF), :] * factor
        out[pl.ds(at, HALF), :] = (mine + half_in[slot].astype(jnp.float32)).astype(jnp.bfloat16)

    def send_outer(d, carry):
        peer = lax.rem(heads - edge + lax.rem(me + d, 2 * edge), heads)
        give(1, peer)
        give(2, peer)
        return carry

    lax.fori_loop(0, 2 * edge, send_outer, 0)

    for n, src, dst in outs:
        pltpu.make_async_copy(src.at[span(me)], dst.at[:, lanes(me)], local.at[n]).wait()

    def finish(d, carry):
        other = lax.rem(me + d, heads)
        for n in range(4):
            in_copy(n, other, me).wait_send()
        for n, src, dst in outs:
            out_copy(n, src, dst, other, me).wait_send()
            out_copy(n, src, dst, other, other).wait_recv()
        return carry

    lax.fori_loop(1, heads, finish, 0)
    for copy in halos + backs:
        copy.wait_send()


def settle(*refs):
    froms, tos, holds = refs[:3], refs[3:6], refs[6:9]
    into, onto = refs[9:]
    reads = [pltpu.make_async_copy(a, b, into.at[i]) for i, (a, b) in enumerate(zip(froms, holds))]
    writes = [pltpu.make_async_copy(b, c, onto.at[i]) for i, (b, c) in enumerate(zip(holds, tos))]
    for read in reads:
        read.start()
    for read, write in zip(reads, writes):
        read.wait()
        write.start()
    for write in writes:
        write.wait()


def shards(query, key_in, value, grad_out):
    heads = lax.axis_size("head")
    blks = lax.axis_size("blk")
    part = query.shape[0]
    rows = heads * part
    wide = rows + 2 * HALF
    bf16, f32 = jnp.bfloat16, jnp.float32
    shape = jax.ShapeDtypeStruct(query.shape, bf16)
    any_spec = pl.BlockSpec(memory_space=pl.ANY)
    dma = pltpu.SemaphoreType.DMA
    grads = pl.pallas_call(
        functools.partial(kernel, heads, blks, part),
        out_shape=(shape, shape, shape),
        in_specs=[any_spec] * 4,
        out_specs=(any_spec,) * 3,
        scratch_shapes=[
            pltpu.VMEM((rows, DIM), bf16),
            pltpu.VMEM((rows, DIM), bf16),
            pltpu.VMEM((wide, DIM), bf16),
            pltpu.VMEM((wide, DIM), bf16),
            pltpu.VMEM((wide // T, DIM, T), bf16),
            pltpu.VMEM((rows // T, CHUNKS, T, T), f32),
            pltpu.VMEM((CHUNKS, T, T), f32),
            pltpu.VMEM((rows // T, 1, T), f32),
            pltpu.VMEM((wide, DIM), f32),
            pltpu.VMEM((wide, DIM), f32),
            pltpu.VMEM((rows, DIM), bf16),
            pltpu.VMEM((rows, DIM), bf16),
            pltpu.VMEM((rows, DIM), bf16),
            pltpu.VMEM((4, HALF, DIM), bf16),
            pltpu.VMEM((4, HALF, DIM), bf16),
            dma((7, heads)),
            dma((7, heads)),
            dma((4,)),
            dma((4,)),
            dma((4,)),
            dma((4,)),
            dma((7,)),
        ],
        compiler_params=pltpu.CompilerParams(collective_id=0, has_side_effects=True),
    )(query, key_in, value, grad_out)
    return pl.pallas_call(
        settle,
        out_shape=(shape, shape, shape),
        in_specs=[any_spec] * 3,
        out_specs=(any_spec,) * 3,
        scratch_shapes=[pltpu.VMEM(query.shape, bf16)] * 3 + [dma((3,)), dma((3,))],
    )(*grads)


def solution(mesh):
    placed = P(("blk", "head"), None)
    return jax.shard_map(
        shards,
        mesh=mesh,
        in_specs=(placed,) * 4,
        out_specs=(placed,) * 3,
        check_vma=False,
    )
```
